256 devices in a mesh: row: 32 (over x_lo, z, core), col: 8 (over x_hi, y).
Axes of the slice: x: 4 (x_hi: 2, x_lo: 2; x = x_hi * 2 + x_lo), y: 4, z: 8, core: 2. Of those that a mesh axis runs over, the one named last changes fastest.
Arguments:
- embeddings: bfloat16 [131072, 768], P(('row', 'col')), may hold values from -7.5 to 7.5
- block_cluster: int32 [512], replicated, may hold values from 0 to 127, never falling along the last dimension, each value on 1 to 8 neighbouring positions
- partner_shift: int32 [131072], P(('row', 'col')), may hold values from 1 to 255
Outputs:
- item_loss: float32 [131072], P(('row', 'col'))
- embedding_grad: float32 [131072, 768], P(('row', 'col'))
The draws below stay inside these ranges and needn't reach their ends.
Inputs may be any that keep to these rules, and one draw needn't show every extreme that they name: block_cluster never falls along the blocks; each value is held by 1 to 8 consecutive blocks, and some value by exactly 8.
All inputs are finite; a program needn't handle non-finite values.
Results may differ from the reference program's by a relative error of at most 0.0018.
Values may be sent and summed in bfloat16 or wider, within the bound.
No kernel may reach another device: no remote copies, remote signals or barrier semaphores. Data moves between devices by JAX's collectives and lax.ppermute only.
A program may use at most 128 MiB of HBM per device.

```python
import math
import jax
import jax.numpy as jnp
import numpy as np
from jax import lax

D = 768
BLOCK = 256
MOST = 8
ITEMS = 131072
BLOCKS = 512
CLUSTERS = 128


def draw_embeddings(key, part):
    k_base, k_scale = jax.random.split(key, 2)
    base = jax.random.normal(k_base, (ITEMS, D), jnp.float32)
    spread = jax.random.uniform(k_scale, (ITEMS, 1), jnp.float32, math.log(0.5), math.log(2.0))
    values = jnp.clip(base * jnp.exp(spread), -7.5, 7.5)
    return values.astype(jnp.bfloat16)


def plant(entries, own_key, least, high):
    longest = entries.shape.index(max(entries.shape))
    spots = []
    for shift in (0, 1):
        where = [jax.random.randint(jax.random.fold_in(own_key, axis), (), 0, length) for axis, length in enumerate(entries.shape)]
        where[longest] = (where[longest] + shift) % entries.shape[longest]
        spots.append(tuple(where))
    return entries.at[spots[0]].set(least).at[spots[1]].set(high)


def length_profile(number_of, total, limit, lean):
    loads = [(1 << 20) // math.isqrt(standing ** lean) + 1 for standing in range(2, number_of + 1)]
    rest, given = total - limit - (number_of - 1), [1] * (number_of - 1)
    while rest > 0:
        movable = [i for i in range(number_of - 1) if given[i] < limit]
        whole, remaining = sum([loads[i] for i in movable]), rest
        for i in movable:
            extra = min(limit - given[i], max(1, remaining * loads[i] // whole), rest)
            given[i] = given[i] + extra
            rest = rest - extra
    return np.array([limit] + given)


def uneven_parts(stream_key, number_of, total, most, slope):
    if number_of == 2:
        one = jax.random.randint(stream_key, (), max(1, total - most), min(most, total - 1) + 1)
        return jnp.stack([one, total - one])
    sizes = jnp.asarray(length_profile(number_of, total, most, slope), jnp.int32)
    couples = (number_of - 1) // 2
    giver, taker = sizes[1:1 + 2 * couples:2], sizes[2:2 + 2 * couples:2]
    room = jnp.minimum(giver - 1, most - taker)
    moved = jax.random.randint(jax.random.fold_in(stream_key, 1), (couples,), 0, 1 << 20) % (room + 1)
    sizes = sizes.at[1:1 + 2 * couples:2].set(giver - moved).at[2:2 + 2 * couples:2].set(taker + moved)
    return sizes[jax.random.permutation(jax.random.fold_in(stream_key, 2), number_of)]


def setup_inputs(seed: int = 0) -> dict:
    key_list = jax.random.split(jax.random.key(seed), 4)
    embeddings = draw_embeddings(jax.random.fold_in(key_list[3], 71), 0)
    block_cluster = jnp.searchsorted(jnp.cumsum(uneven_parts(key_list[1], CLUSTERS, BLOCKS, MOST, 2)), jnp.arange(BLOCKS), side="right").astype(jnp.int32)
    partner_shift = plant(jax.random.randint(key_list[2], (ITEMS,), 1, BLOCK), jax.random.fold_in(key_list[2], 1), 1, BLOCK - 1).astype(jnp.int32)
    return {"embeddings": embeddings, "block_cluster": block_cluster, "partner_shift": partner_shift}


NEG = -1.0e30


def shift_blocks(values, offset):
    if offset == 0:
        return values
    pad = jnp.zeros((abs(offset),) + values.shape[1:], values.dtype)
    if offset > 0:
        return jnp.concatenate([values[offset:], pad], 0)
    return jnp.concatenate([pad, values[:offset]], 0)


def reference(embeddings, block_cluster, partner_shift):
    nblocks = ITEMS // BLOCK
    scale = D ** -0.5
    span = MOST - 1
    blocked = embeddings.astype(jnp.float32).reshape(nblocks, BLOCK, D)
    index = jnp.arange(nblocks, dtype=jnp.int32)
    position = jnp.arange(BLOCK, dtype=jnp.int32)
    diagonal = position[:, None] == position[None, :]

    def live_at(offset):
        valid = (index + offset >= 0) & (index + offset < nblocks)
        same = block_cluster == shift_blocks(block_cluster, offset)
        live = jnp.broadcast_to((valid & same)[:, None, None], (nblocks, BLOCK, BLOCK))
        if offset == 0:
            live = live & jnp.logical_not(diagonal)[None]
        return live

    def scores_at(offset):
        partner = shift_blocks(blocked, offset)
        return jnp.einsum("abd,acd->abc", blocked, partner, precision=lax.Precision.HIGHEST) * scale

    top = jnp.full((nblocks, BLOCK), NEG, jnp.float32)
    total = jnp.zeros((nblocks, BLOCK), jnp.float32)
    for offset in range(-span, span + 1):
        live = live_at(offset)
        masked = jnp.where(live, scores_at(offset), NEG)
        new_top = jnp.maximum(top, jnp.max(masked, axis=2))
        total = total * jnp.exp(top - new_top) + jnp.sum(jnp.where(live, jnp.exp(masked - new_top[:, :, None]), 0.0), axis=2)
        top = new_top
    lse = top + jnp.log(total)

    shifts = partner_shift.reshape(nblocks, BLOCK)
    partner = (position[None, :] + shifts) % BLOCK
    positive = position[None, None, :] == partner[:, :, None]
    self_scores = scores_at(0)
    loss = lse - jnp.sum(jnp.where(positive, self_scores, 0.0), axis=2)

    grad = jnp.zeros((nblocks, BLOCK, D), jnp.float32)
    for offset in range(-span, span + 1):
        live = live_at(offset)
        scores = scores_at(offset)
        rowwise = jnp.exp(jnp.where(live, scores - lse[:, :, None], NEG))
        if offset == 0:
            rowwise = rowwise - positive.astype(jnp.float32)
            both = rowwise + jnp.swapaxes(rowwise, 1, 2)
        else:
            far = shift_blocks(lse, offset)
            both = rowwise + jnp.exp(jnp.where(live, scores - far[:, None, :], NEG))
        weights = lax.optimization_barrier(both.astype(jnp.bfloat16)).astype(jnp.float32)
        grad = grad + jnp.einsum("abc,acd->abd", weights, shift_blocks(blocked, offset), precision=lax.Precision.HIGHEST) * scale
    return loss.reshape(ITEMS), grad.reshape(ITEMS, D)
```

```python
import functools
import math

import jax
import jax.numpy as jnp
from jax import lax
from jax.experimental import pallas as pl
from jax.experimental.pallas import tpu as pltpu
from jax.sharding import PartitionSpec as P

BLOCK = 256
REACH = 4
MOST = 8
NEG = -1e30
AXES = ("row", "col")


def shifted(value, steps):
    count = lax.axis_size(AXES)
    leading, last = (max(0, -steps), min(count, count - steps))
    return lax.ppermute(value, AXES, [(source, source + steps) for source in range(leading, last)])


def kernel(dev_ref, cluster_ref, shift_ref, *refs):
    slabs = refs[: 2 * REACH + 1]
    loss_ref, grad_ref, window, scores, lse, weights, sems = refs[2 * REACH + 1 :]
    rows, width = slabs[0].shape
    here = rows // BLOCK
    blocks = cluster_ref.shape[0]
    scale = width**-0.5
    log2e = math.log2(math.e)
    copies = [
        pltpu.make_async_copy(slab, window.at[pl.ds(n * rows, rows), :], sems.at[n])
        for n, slab in enumerate(slabs)
    ]
    for copy in copies:
        copy.start()

    first = dev_ref[0] * here - REACH * here

    def cluster_at(w):
        g = first + w
        inside = jnp.logical_and(g >= 0, g < blocks)
        return jnp.where(inside, cluster_ref[jnp.clip(g, 0, blocks - 1)], -1)

    def extent(own):
        mine = cluster_at(own)
        begin, end = jnp.int32(own), jnp.int32(own + 1)
        for step in range(1, MOST):
            begin = jnp.where(cluster_at(own - step) == mine, own - step, begin)
            end = jnp.where(cluster_at(own + step) == mine, own + step + 1, end)
        return begin, end

    begin0, end0 = extent(REACH * here)
    begin1, end1 = extent(REACH * here + 1)
    for copy in copies:
        copy.wait()

    row = lax.broadcasted_iota(jnp.int32, (BLOCK, BLOCK), 0)
    column = lax.broadcasted_iota(jnp.int32, (BLOCK, BLOCK), 1)
    span = MOST * BLOCK

    def at(block):
        return pl.ds(pl.multiple_of(block * BLOCK, BLOCK), BLOCK)

    def upright(values):
        return jnp.sum(jnp.where(row == column, values, 0.0), axis=1, keepdims=True)

    def own_block(r, _):
        begin = jnp.where(r == 0, begin0, begin1)
        length = jnp.where(r == 0, end0, end1) - begin
        own = REACH * here + r - begin

        def statistics(j, _):
            far = window[at(begin + j), :]
            for i in range(MOST):
                tile = lax.dot_general(
                    window[at(begin + i), :],
                    far,
                    (((1,), (1,)), ((), ())),
                    preferred_element_type=jnp.float32,
                )
                scores[j, i * BLOCK : (i + 1) * BLOCK, :] = tile * (scale * log2e)
            scores[j, at(j), :] = jnp.where(row == column, NEG, scores[j, at(j), :])
            top = jnp.full((8, BLOCK), NEG, jnp.float32)
            for i in range(MOST):
                tile = scores[j, i * BLOCK : (i + 1) * BLOCK, :]
                part = jnp.max(tile.reshape(BLOCK // 8, 8, BLOCK), axis=0)
                top = jnp.where(i < length, jnp.maximum(top, part), top)
            top = jnp.max(top, axis=0, keepdims=True)
            total = jnp.zeros((8, BLOCK), jnp.float32)
            for i in range(MOST):
                tile = jnp.exp2(scores[j, i * BLOCK : (i + 1) * BLOCK, :] - top)
                part = jnp.sum(tile.reshape(BLOCK // 8, 8, BLOCK), axis=0)
                total = jnp.where(i < length, total + part, total)
            lse[pl.ds(j, 1), :] = top + jnp.log2(jnp.sum(total, axis=0, keepdims=True))
            return 0

        @pl.when(jnp.logical_or(r == 0, begin0 != begin1))
        def _():
            lax.fori_loop(0, length, statistics, 0)

        mine = lse[pl.ds(own, 1), :]
        mine_up = upright(mine)

        def weigh(j, _):
            tile = scores[j, at(own), :]
            weight = jnp.exp2(tile - mine_up) + jnp.exp2(tile - lse[pl.ds(j, 1), :])
            weights[:, at(j)] = weight.astype(jnp.bfloat16)
            return 0

        def blank(j, _):
            weights[:, at(j)] = jnp.zeros((BLOCK, BLOCK), jnp.bfloat16)
            return 0

        lax.fori_loop(0, length, weigh, 0)
        lax.fori_loop(length, MOST, blank, 0)
        shift = shift_ref[pl.ds(r, 1), :]
        shift_up = upright(shift.astype(jnp.float32)).astype(jnp.int32)
        tile = scores[own, at(own), :]
        behind = row == jnp.bitwise_and(column + shift, BLOCK - 1)
        ahead = column == jnp.bitwise_and(row + shift_up, BLOCK - 1)
        weight = jnp.exp2(tile - mine_up) + jnp.exp2(tile - mine)
        weight = weight - jnp.where(ahead, 1.0, 0.0) - jnp.where(behind, 1.0, 0.0)
        weights[:, at(own)] = weight.astype(jnp.bfloat16)
        positive = jnp.sum(jnp.where(behind, tile, 0.0), axis=0, keepdims=True)
        loss_ref[pl.ds(r, 1), :] = (mine - positive) * (1.0 / log2e)
        total = jnp.dot(
            weights[...],
            window[pl.ds(pl.multiple_of(begin * BLOCK, BLOCK), span), :],
            preferred_element_type=jnp.float32,
        )
        grad_ref[at(r), :] = total * scale
        return 0

    lax.fori_loop(0, here, own_block, 0)


def local_work(device, block_cluster, partner_shift, slabs):
    rows, width = slabs[0].shape
    here = rows // BLOCK
    whole = pl.BlockSpec(memory_space=pltpu.VMEM)
    scalar = pl.BlockSpec(memory_space=pltpu.SMEM)
    loss, grad = pl.pallas_call(
        kernel,
        out_shape=(
            jax.ShapeDtypeStruct((here, BLOCK), jnp.float32),
            jax.ShapeDtypeStruct((rows, width), jnp.float32),
        ),
        in_specs=[scalar, scalar, whole] + [pl.BlockSpec(memory_space=pl.ANY)] * len(slabs),
        out_specs=(whole, whole),
        scratch_shapes=[
            pltpu.VMEM((len(slabs) * rows, width), jnp.bfloat16),
            pltpu.VMEM((MOST, MOST * BLOCK, BLOCK), jnp.float32),
            pltpu.VMEM((MOST, BLOCK), jnp.float32),
            pltpu.VMEM((BLOCK, MOST * BLOCK), jnp.bfloat16),
            pltpu.SemaphoreType.DMA((len(slabs),)),
        ],
        compiler_params=pltpu.CompilerParams(vmem_limit_bytes=48 * 1024 * 1024),
        name="cluster_loss",
    )(device, block_cluster, partner_shift.reshape(here, BLOCK), *slabs)
    return loss.reshape(rows), grad


def shards(embeddings, block_cluster, partner_shift):
    device = lax.axis_index(AXES).astype(jnp.int32).reshape(1)
    slabs = [
        embeddings if offset == 0 else shifted(embeddings, -offset)
        for offset in range(-REACH, REACH + 1)
    ]
    return local_work(device, block_cluster, partner_shift, slabs)


def solution(mesh):
    in_specs = (P(AXES, None), P(), P(AXES))
    out_specs = (P(AXES), P(AXES, None))
    return jax.shard_map(shards, mesh=mesh, in_specs=in_specs, out_specs=out_specs, check_vma=False)
```

```python
import functools
import math

import jax
import jax.numpy as jnp
from jax import lax
from jax.experimental import pallas as pl
from jax.experimental.pallas import tpu as pltpu
from jax.sharding import PartitionSpec as P

BLOCK = 256
REACH = 4
LINE = 4
MOST = 8
NEG = -1e30
AXES = ("row", "col")


def moved(value, target):
    count = lax.axis_size(AXES)
    pairs = [(source, target(source // LINE, source % LINE)) for source in range(count)]
    pairs = [(source, line * LINE + place) for source, (line, place) in pairs]
    return lax.ppermute(value, AXES, [(s, t) for s, t in pairs if 0 <= t < count])


def around(value, steps):
    return moved(value, lambda line, place: (line, (place + steps) % LINE))


def exchange(own, place):
    late = moved(own, lambda line, place: (line + 1 if place == LINE - 1 else line - 1, place))
    early = moved(own, lambda line, place: (line - 1 if place == LINE - 1 else line + 1, place))
    across = around(own, 2)
    up = around(own, 1)
    down = around(own, -1)
    crossed = moved(across, lambda line, place: (line - 1 if place >= 2 else line + 1, place))
    late_up = around(late, 1)
    inner = jnp.logical_or(place == 1, place == 2)
    early_down = around(jnp.where(inner, early, late), -1)
    return [own, late, early, across, up, down, crossed, late_up, early_down]


def slots(place):
    late = jnp.where(place < 3, 8, 0)
    across = jnp.where(place >= 2, 2, 6)
    up = jnp.where(place >= 1, 3, 7)
    down = jnp.where(place <= 2, 5, 1)
    return [4, late, 8 - late, across, up, down, 8 - across, 10 - up, 6 - down]


def kernel(dev_ref, cluster_ref, shift_ref, *refs):
    slabs = refs[: 2 * REACH + 1]
    loss_ref, grad_ref, window, scores, lse, weights, sems = refs[2 * REACH + 1 :]
    rows, width = slabs[0].shape
    here = rows // BLOCK
    blocks = cluster_ref.shape[0]
    scale = width**-0.5
    log2e = math.log2(math.e)
    places = slots(lax.rem(dev_ref[0], LINE))
    copies = [
        pltpu.make_async_copy(
            slab, window.at[pl.ds(pl.multiple_of(place * rows, rows), rows), :], sems.at[n]
        )
        for n, (slab, place) in enumerate(zip(slabs, places))
    ]
    for copy in copies:
        copy.start()

    first = dev_ref[0] * here - REACH * here

    def cluster_at(w):
        g = first + w
        inside = jnp.logical_and(g >= 0, g < blocks)
        return jnp.where(inside, cluster_ref[jnp.clip(g, 0, blocks - 1)], -1)

    def extent(own):
        mine = cluster_at(own)
        begin, end = jnp.int32(own), jnp.int32(own + 1)
        for step in range(1, MOST):
            begin = jnp.where(cluster_at(own - step) == mine, own - step, begin)
            end = jnp.where(cluster_at(own + step) == mine, own + step + 1, end)
        return begin, end

    begin0, end0 = extent(REACH * here)
    begin1, end1 = extent(REACH * here + 1)
    for copy in copies:
        copy.wait()

    row = lax.broadcasted_iota(jnp.int32, (BLOCK, BLOCK), 0)
    column = lax.broadcasted_iota(jnp.int32, (BLOCK, BLOCK), 1)
    span = MOST * BLOCK

    def at(block):
        return pl.ds(pl.multiple_of(block * BLOCK, BLOCK), BLOCK)

    def upright(values):
        return jnp.sum(jnp.where(row == column, values, 0.0), axis=1, keepdims=True)

    def own_block(r, _):
        begin = jnp.where(r == 0, begin0, begin1)
        length = jnp.where(r == 0, end0, end1) - begin
        own = REACH * here + r - begin

        def statistics(j, _):
            far = window[at(begin + j), :]
            for i in range(MOST):
                tile = lax.dot_general(
                    window[at(begin + i), :],
                    far,
                    (((1,), (1,)), ((), ())),
                    preferred_element_type=jnp.float32,
                )
                scores[j, i * BLOCK : (i + 1) * BLOCK, :] = tile * (scale * log2e)
            scores[j, at(j), :] = jnp.where(row == column, NEG, scores[j, at(j), :])
            top = jnp.full((8, BLOCK), NEG, jnp.float32)
            for i in range(MOST):
                tile = scores[j, i * BLOCK : (i + 1) * BLOCK, :]
                part = jnp.max(tile.reshape(BLOCK // 8, 8, BLOCK), axis=0)
                top = jnp.where(i < length, jnp.maximum(top, part), top)
            top = jnp.max(top, axis=0, keepdims=True)
            total = jnp.zeros((8, BLOCK), jnp.float32)
            for i in range(MOST):
                tile = jnp.exp2(scores[j, i * BLOCK : (i + 1) * BLOCK, :] - top)
                part = jnp.sum(tile.reshape(BLOCK // 8, 8, BLOCK), axis=0)
                total = jnp.where(i < length, total + part, total)
            lse[pl.ds(j, 1), :] = top + jnp.log2(jnp.sum(total, axis=0, keepdims=True))
            return 0

        @pl.when(jnp.logical_or(r == 0, begin0 != begin1))
        def _():
            lax.fori_loop(0, length, statistics, 0)

        mine = lse[pl.ds(own, 1), :]
        mine_up = upright(mine)

        def weigh(j, _):
            tile = scores[j, at(own), :]
            weight = jnp.exp2(tile - mine_up) + jnp.exp2(tile - lse[pl.ds(j, 1), :])
            weights[:, at(j)] = weight.astype(jnp.bfloat16)
            return 0

        def blank(j, _):
            weights[:, at(j)] = jnp.zeros((BLOCK, BLOCK), jnp.bfloat16)
            return 0

        lax.fori_loop(0, length, weigh, 0)
        lax.fori_loop(length, MOST, blank, 0)
        shift = shift_ref[pl.ds(r, 1), :]
        shift_up = upright(shift.astype(jnp.float32)).astype(jnp.int32)
        tile = scores[own, at(own), :]
        behind = row == jnp.bitwise_and(column + shift, BLOCK - 1)
        ahead = column == jnp.bitwise_and(row + shift_up, BLOCK - 1)
        weight = jnp.exp2(tile - mine_up) + jnp.exp2(tile - mine)
        weight = weight - jnp.where(ahead, 1.0, 0.0) - jnp.where(behind, 1.0, 0.0)
        weights[:, at(own)] = weight.astype(jnp.bfloat16)
        positive = jnp.sum(jnp.where(behind, tile, 0.0), axis=0, keepdims=True)
        loss_ref[pl.ds(r, 1), :] = (mine - positive) * (1.0 / log2e)
        total = jnp.dot(
            weights[...],
            window[pl.ds(pl.multiple_of(begin * BLOCK, BLOCK), span), :],
            preferred_element_type=jnp.float32,
        )
        grad_ref[at(r), :] = total * scale
        return 0

    lax.fori_loop(0, here, own_block, 0)


def local_work(device, block_cluster, partner_shift, slabs):
    rows, width = slabs[0].shape
    here = rows // BLOCK
    whole = pl.BlockSpec(memory_space=pltpu.VMEM)
    scalar = pl.BlockSpec(memory_space=pltpu.SMEM)
    loss, grad = pl.pallas_call(
        kernel,
        out_shape=(
            jax.ShapeDtypeStruct((here, BLOCK), jnp.float32),
            jax.ShapeDtypeStruct((rows, width), jnp.float32),
        ),
        in_specs=[scalar, scalar, whole] + [pl.BlockSpec(memory_space=pl.ANY)] * len(slabs),
        out_specs=(whole, whole),
        scratch_shapes=[
            pltpu.VMEM((len(slabs) * rows, width), jnp.bfloat16),
            pltpu.VMEM((MOST, MOST * BLOCK, BLOCK), jnp.float32),
            pltpu.VMEM((MOST, BLOCK), jnp.float32),
            pltpu.VMEM((BLOCK, MOST * BLOCK), jnp.bfloat16),
            pltpu.SemaphoreType.DMA((len(slabs),)),
        ],
        compiler_params=pltpu.CompilerParams(vmem_limit_bytes=48 * 1024 * 1024),
        name="cluster_loss",
    )(device, block_cluster, partner_shift.reshape(here, BLOCK), *slabs)
    return loss.reshape(rows), grad


def shards(embeddings, block_cluster, partner_shift):
    device = lax.axis_index(AXES).astype(jnp.int32).reshape(1)
    slabs = exchange(embeddings, lax.rem(lax.axis_index("col"), LINE))
    return local_work(device, block_cluster, partner_shift, slabs)


def solution(mesh):
    in_specs = (P(AXES, None), P(), P(AXES))
    out_specs = (P(AXES), P(AXES, None))
    return jax.shard_map(shards, mesh=mesh, in_specs=in_specs, out_specs=out_specs, check_vma=False)
```

```python
import functools
import math

import jax
import jax.numpy as jnp
from jax import lax
from jax.experimental import pallas as pl
from jax.experimental.pallas import tpu as pltpu
from jax.sharding import PartitionSpec as P

BLOCK = 256
REACH = 4
LINE = 4
MOST = 8
NEG = -1e30
AXES = ("row", "col")


def moved(value, target):
    count = lax.axis_size(AXES)
    pairs = [(source, target(source // LINE, source % LINE)) for source in range(count)]
    pairs = [(source, (line * LINE + place) % count) for source, (line, place) in pairs]
    return lax.ppermute(value, AXES, pairs)


def around(value, steps):
    return moved(value, lambda line, place: (line, (place + steps) % LINE))


def exchange(own, place):
    late = moved(own, lambda line, place: (line + 1 if place == LINE - 1 else line - 1, place))
    across = around(own, 2)
    up = around(own, 1)
    down = around(own, -1)
    early = moved(late, lambda line, place: (line - 2 if place == LINE - 1 else line + 2, place))
    crossed = moved(across, lambda line, place: (line - 1 if place >= 2 else line + 1, place))
    late_up = around(late, 1)
    inner = jnp.logical_or(place == 1, place == 2)
    early_down = around(jnp.where(inner, early, late), -1)
    return [own, late, early, across, up, down, crossed, late_up, early_down]


def slots(place):
    late = jnp.where(place < 3, 8, 0)
    across = jnp.where(place >= 2, 2, 6)
    up = jnp.where(place >= 1, 3, 7)
    down = jnp.where(place <= 2, 5, 1)
    return [4, late, 8 - late, across, up, down, 8 - across, 10 - up, 6 - down]


def kernel(dev_ref, cluster_ref, shift_ref, *refs):
    slabs = refs[: 2 * REACH + 1]
    loss_ref, grad_ref, window, scores, lse, weights, sems = refs[2 * REACH + 1 :]
    rows, width = slabs[0].shape
    here = rows // BLOCK
    blocks = cluster_ref.shape[0]
    scale = width**-0.5
    log2e = math.log2(math.e)
    places = slots(lax.rem(dev_ref[0], LINE))
    copies = [
        pltpu.make_async_copy(
            slab, window.at[pl.ds(pl.multiple_of(place * rows, rows), rows), :], sems.at[n]
        )
        for n, (slab, place) in enumerate(zip(slabs, places))
    ]
    for copy in copies:
        copy.start()

    first = dev_ref[0] * here - REACH * here

    def cluster_at(w):
        g = first + w
        inside = jnp.logical_and(g >= 0, g < blocks)
        return jnp.where(inside, cluster_ref[jnp.clip(g, 0, blocks - 1)], -1)

    def extent(own):
        mine = cluster_at(own)
        begin, end = jnp.int32(own), jnp.int32(own + 1)
        for step in range(1, MOST):
            begin = jnp.where(cluster_at(own - step) == mine, own - step, begin)
            end = jnp.where(cluster_at(own + step) == mine, own + step + 1, end)
        return begin, end

    begin0, end0 = extent(REACH * here)
    begin1, end1 = extent(REACH * here + 1)
    for copy in copies:
        copy.wait()

    row = lax.broadcasted_iota(jnp.int32, (BLOCK, BLOCK), 0)
    column = lax.broadcasted_iota(jnp.int32, (BLOCK, BLOCK), 1)
    span = MOST * BLOCK

    def at(block):
        return pl.ds(pl.multiple_of(block * BLOCK, BLOCK), BLOCK)

    def upright(values):
        return jnp.sum(jnp.where(row == column, values, 0.0), axis=1, keepdims=True)

    def own_block(r, _):
        begin = jnp.where(r == 0, begin0, begin1)
        length = jnp.where(r == 0, end0, end1) - begin
        own = REACH * here + r - begin

        def statistics(j, _):
            far = window[at(begin + j), :]
            for i in range(MOST):
                tile = lax.dot_general(
                    window[at(begin + i), :],
                    far,
                    (((1,), (1,)), ((), ())),
                    preferred_element_type=jnp.float32,
                )
                scores[j, i * BLOCK : (i + 1) * BLOCK, :] = tile * (scale * log2e)
            scores[j, at(j), :] = jnp.where(row == column, NEG, scores[j, at(j), :])
            top = jnp.full((8, BLOCK), NEG, jnp.float32)
            for i in range(MOST):
                tile = scores[j, i * BLOCK : (i + 1) * BLOCK, :]
                part = jnp.max(tile.reshape(BLOCK // 8, 8, BLOCK), axis=0)
                top = jnp.where(i < length, jnp.maximum(top, part), top)
            top = jnp.max(top, axis=0, keepdims=True)
            total = jnp.zeros((8, BLOCK), jnp.float32)
            for i in range(MOST):
                tile = jnp.exp2(scores[j, i * BLOCK : (i + 1) * BLOCK, :] - top)
                part = jnp.sum(tile.reshape(BLOCK // 8, 8, BLOCK), axis=0)
                total = jnp.where(i < length, total + part, total)
            lse[pl.ds(j, 1), :] = top + jnp.log2(jnp.sum(total, axis=0, keepdims=True))
            return 0

        @pl.when(jnp.logical_or(r == 0, begin0 != begin1))
        def _():
            lax.fori_loop(0, length, statistics, 0)

        mine = lse[pl.ds(own, 1), :]
        mine_up = upright(mine)

        def weigh(j, _):
            tile = scores[j, at(own), :]
            weight = jnp.exp2(tile - mine_up) + jnp.exp2(tile - lse[pl.ds(j, 1), :])
            weights[:, at(j)] = weight.astype(jnp.bfloat16)
            return 0

        def blank(j, _):
            weights[:, at(j)] = jnp.zeros((BLOCK, BLOCK), jnp.bfloat16)
            return 0

        lax.fori_loop(0, length, weigh, 0)
        lax.fori_loop(length, MOST, blank, 0)
        shift = shift_ref[pl.ds(r, 1), :]
        shift_up = upright(shift.astype(jnp.float32)).astype(jnp.int32)
        tile = scores[own, at(own), :]
        behind = row == jnp.bitwise_and(column + shift, BLOCK - 1)
        ahead = column == jnp.bitwise_and(row + shift_up, BLOCK - 1)
        weight = jnp.exp2(tile - mine_up) + jnp.exp2(tile - mine)
        weight = weight - jnp.where(ahead, 1.0, 0.0) - jnp.where(behind, 1.0, 0.0)
        weights[:, at(own)] = weight.astype(jnp.bfloat16)
        positive = jnp.sum(jnp.where(behind, tile, 0.0), axis=0, keepdims=True)
        loss_ref[pl.ds(r, 1), :] = (mine - positive) * (1.0 / log2e)
        total = jnp.dot(
            weights[...],
            window[pl.ds(pl.multiple_of(begin * BLOCK, BLOCK), span), :],
            preferred_element_type=jnp.float32,
        )
        grad_ref[at(r), :] = total * scale
        return 0

    lax.fori_loop(0, here, own_block, 0)


def local_work(device, block_cluster, partner_shift, slabs):
    rows, width = slabs[0].shape
    here = rows // BLOCK
    whole = pl.BlockSpec(memory_space=pltpu.VMEM)
    scalar = pl.BlockSpec(memory_space=pltpu.SMEM)
    loss, grad = pl.pallas_call(
        kernel,
        out_shape=(
            jax.ShapeDtypeStruct((here, BLOCK), jnp.float32),
            jax.ShapeDtypeStruct((rows, width), jnp.float32),
        ),
        in_specs=[scalar, scalar, whole] + [pl.BlockSpec(memory_space=pl.ANY)] * len(slabs),
        out_specs=(whole, whole),
        scratch_shapes=[
            pltpu.VMEM((len(slabs) * rows, width), jnp.bfloat16),
            pltpu.VMEM((MOST, MOST * BLOCK, BLOCK), jnp.float32),
            pltpu.VMEM((MOST, BLOCK), jnp.float32),
            pltpu.VMEM((BLOCK, MOST * BLOCK), jnp.bfloat16),
            pltpu.SemaphoreType.DMA((len(slabs),)),
        ],
        compiler_params=pltpu.CompilerParams(vmem_limit_bytes=48 * 1024 * 1024),
        name="cluster_loss",
    )(device, block_cluster, partner_shift.reshape(here, BLOCK), *slabs)
    return loss.reshape(rows), grad


def shards(embeddings, block_cluster, partner_shift):
    device = lax.axis_index(AXES).astype(jnp.int32).reshape(1)
    slabs = exchange(embeddings, lax.rem(lax.axis_index("col"), LINE))
    return local_work(device, block_cluster, partner_shift, slabs)


def solution(mesh):
    in_specs = (P(AXES, None), P(), P(AXES))
    out_specs = (P(AXES), P(AXES, None))
    return jax.shard_map(shards, mesh=mesh, in_specs=in_specs, out_specs=out_specs, check_vma=False)
```

```python
import functools
import math

import jax
import jax.numpy as jnp
from jax import lax
from jax.experimental import pallas as pl
from jax.experimental.pallas import tpu as pltpu
from jax.sharding import PartitionSpec as P

BLOCK = 256
REACH = 4
LINE = 4
MOST = 8
NEG = -1e30
AXES = ("row", "col")


def moved(value, target):
    count = lax.axis_size(AXES)
    pairs = [(source, target(source // LINE, source % LINE)) for source in range(count)]
    pairs = [(source, to[0] * LINE + to[1]) for source, to in pairs if to is not None]
    return lax.ppermute(value, AXES, [(source, to % count) for source, to in pairs])


def parity(line):
    return line // 2 % 2


def exchange(own, *ready):
    late = moved(own, lambda line, at: (line + 1 if at == LINE - 1 else line - 1, at))
    near = moved(own, lambda line, at: (line, (at + (1 if (at + parity(line)) % 2 else -1)) % LINE))
    other = moved(own, lambda line, at: (line, (at - (1 if (at + parity(line)) % 2 else -1)) % LINE))
    across = moved(near, lambda line, at: (line, (at - (1 if (at + parity(line)) % 2 else -1)) % LINE))
    late_sent, *ready = lax.optimization_barrier((late, *ready))
    early = moved(late_sent, lambda line, at: (line - 2 if at == LINE - 1 else line + 2, at))
    late_up = moved(late, lambda line, at: (line, (at + 1) % LINE))
    late_down = moved(late, lambda line, at: (line, at - 1) if at == 3 else (line, 3) if at == 0 else None)
    early_down = moved(early, lambda line, at: (line, at - 1) if at in (1, 2) else None)
    crossed = moved(across, lambda line, at: (line - 1 if at >= 2 else line + 1, at))
    slabs = [own, late, early, across, near, other, crossed, late_up, late_down, early_down]
    return slabs, ready


def slots(device):
    at = lax.rem(device, LINE)
    late = jnp.where(at < 3, 8, 0)
    across = jnp.where(at >= 2, 2, 6)
    from_before = jnp.where(at >= 1, 3, 7)
    from_after = jnp.where(at <= 2, 5, 1)
    before = lax.rem(at + lax.rem(lax.div(device, 2 * LINE), 2), 2) == 0
    near = jnp.where(before, from_before, from_after)
    other = jnp.where(before, from_after, from_before)
    down = 6 - from_after
    where = [4, late, 8 - late, across, near, other, 8 - across, 10 - from_before, down, down]
    return where, [None] * 8 + [at >= 2, at < 2]


def stage(here, new_slots, prior_slots, first, last, refs):
    info_ref, refs = refs[0], refs[1:]
    slabs, refs = refs[: len(new_slots)], refs[len(new_slots) :]
    if last:
        shift_ref, refs = refs[0], refs[1:]
    if not first:
        refs = refs[4:]
    if last:
        loss_ref, grad_ref, refs = refs[0], refs[1], refs[2:]
    window, kept, tops, totals, scores, sems = refs[:6]
    if last:
        lse, weights = refs[6:]
    rows, width = slabs[0].shape
    scale = width**-0.5
    log2e = math.log2(math.e)
    all_slots, taken = slots(info_ref[0])
    copies = [
        pltpu.make_async_copy(
            slab,
            window.at[pl.ds(pl.multiple_of(all_slots[n] * rows, rows), rows), :],
            sems.at[k],
        )
        for k, (slab, n) in enumerate(zip(slabs, new_slots))
    ]
    copies = [(taken[n], copy) for n, copy in zip(new_slots, copies)]

    def each(act):
        for wanted, copy in copies:
            if wanted is None:
                act(copy)
            else:
                pl.when(wanted)(lambda copy=copy: act(copy))

    each(lambda copy: copy.start())

    def mask_of(ids):
        mask = jnp.int32(0)
        for n in ids:
            mask = jnp.bitwise_or(mask, lax.shift_left(jnp.int32(1), jnp.int32(all_slots[n])))
        return mask

    new_mask, prior_mask = mask_of(new_slots), mask_of(prior_slots)

    def held(mask, w):
        return jnp.bitwise_and(lax.shift_right_logical(mask, lax.div(w, here)), 1) == 1

    begin0, end0, begin1, end1 = [info_ref[n] for n in range(1, 5)]
    each(lambda copy: copy.wait())

    row = lax.broadcasted_iota(jnp.int32, (BLOCK, BLOCK), 0)
    column = lax.broadcasted_iota(jnp.int32, (BLOCK, BLOCK), 1)
    span = MOST * BLOCK
    same = begin0 == begin1

    def at(block):
        return pl.ds(pl.multiple_of(block * BLOCK, BLOCK), BLOCK)

    def folded(op, tile):
        return op(tile.reshape(BLOCK // 8, 8, BLOCK), axis=0)

    def upright(values):
        return jnp.sum(jnp.where(row == column, values, 0.0), axis=1, keepdims=True)

    def product(left, right):
        return lax.dot_general(
            window[at(left), :],
            window[at(right), :],
            (((1,), (1,)), ((), ())),
            preferred_element_type=jnp.float32,
        ) * (scale * log2e)

    def own_block(r, _):
        begin = jnp.where(r == 0, begin0, begin1)
        length = jnp.where(r == 0, end0, end1) - begin
        own = REACH * here + r - begin

        def live(i, mask):
            return jnp.logical_and(i < length, held(mask, begin + i))

        def column_strip(j, _):
            @pl.when(held(new_mask, begin + j))
            def _():
                for i in range(MOST):
                    scores[i * BLOCK : (i + 1) * BLOCK, :] = product(begin + i, begin + j)
                scores[at(j), :] = jnp.where(row == column, NEG, scores[at(j), :])
                top = jnp.full((8, BLOCK), NEG, jnp.float32)
                for i in range(MOST):
                    part = folded(jnp.max, scores[i * BLOCK : (i + 1) * BLOCK, :])
                    there = live(i, new_mask + prior_mask)
                    top = jnp.where(there, jnp.maximum(top, part), top)
                top = jnp.max(top, axis=0, keepdims=True)
                total = jnp.zeros((8, BLOCK), jnp.float32)
                for i in range(MOST):
                    part = folded(jnp.sum, jnp.exp2(scores[i * BLOCK : (i + 1) * BLOCK, :] - top))
                    there = live(i, new_mask + prior_mask)
                    total = jnp.where(there, total + part, total)
                tops[pl.ds(r * MOST + j, 1), :] = top
                totals[pl.ds(r * MOST + j, 1), :] = jnp.sum(total, axis=0, keepdims=True)
                kept[r, j] = scores[at(own), :]

                @pl.when(same)
                def _():
                    kept[1, j] = scores[at(own + 1), :]

                if first:
                    return
                for i in range(MOST):

                    @pl.when(live(i, prior_mask))
                    def _():
                        tile = scores[i * BLOCK : (i + 1) * BLOCK, :].T
                        line = pl.ds(r * MOST + i, 1)
                        old = tops[line, :]
                        part = jnp.max(folded(jnp.max, tile), axis=0, keepdims=True)
                        top = jnp.maximum(old, part)
                        part = jnp.sum(folded(jnp.sum, jnp.exp2(tile - top)), axis=0, keepdims=True)
                        totals[line, :] = totals[line, :] * jnp.exp2(old - top) + part
                        tops[line, :] = top

            return 0

        @pl.when(jnp.logical_or(r == 0, jnp.logical_not(same)))
        def _():
            lax.fori_loop(0, length, column_strip, 0)

        if not last:
            return 0

        base = jnp.where(same, 0, r * MOST)
        ready = pl.ds(pl.multiple_of(base, MOST), MOST)
        lse[...] = tops[ready, :] + jnp.log2(totals[ready, :])
        mine = lse[pl.ds(own, 1), :]
        mine_up = upright(mine)

        def weigh(j, _):
            tile = kept[r, j]
            weight = jnp.exp2(tile - mine_up) + jnp.exp2(tile - lse[pl.ds(j, 1), :])
            weights[:, at(j)] = weight.astype(jnp.bfloat16)
            return 0

        def blank(j, _):
            weights[:, at(j)] = jnp.zeros((BLOCK, BLOCK), jnp.bfloat16)
            return 0

        lax.fori_loop(0, length, weigh, 0)
        lax.fori_loop(length, MOST, blank, 0)
        shift = shift_ref[pl.ds(r, 1), :]
        shift_up = upright(shift.astype(jnp.float32)).astype(jnp.int32)
        tile = kept[r, own]
        behind = row == jnp.bitwise_and(column + shift, BLOCK - 1)
        ahead = column == jnp.bitwise_and(row + shift_up, BLOCK - 1)
        weight = jnp.exp2(tile - mine_up) + jnp.exp2(tile - mine)
        weight = weight - jnp.where(ahead, 1.0, 0.0) - jnp.where(behind, 1.0, 0.0)
        weights[:, at(own)] = weight.astype(jnp.bfloat16)
        positive = jnp.sum(jnp.where(behind, tile, 0.0), axis=0, keepdims=True)
        loss_ref[pl.ds(r, 1), :] = (mine - positive) * (1.0 / log2e)
        total = jnp.dot(
            weights[...],
            window[pl.ds(pl.multiple_of(begin * BLOCK, BLOCK), span), :],
            preferred_element_type=jnp.float32,
        )
        grad_ref[at(r), :] = total * scale
        return 0

    lax.fori_loop(0, here, own_block, 0)


def run_stage(info, slabs, new_slots, prior_slots, state, shifts):
    rows, width = slabs[0].shape
    here = rows // BLOCK
    first, last = state is None, shifts is not None
    whole = pl.BlockSpec(memory_space=pltpu.VMEM)
    scalar = pl.BlockSpec(memory_space=pltpu.SMEM)
    state_shape = [
        pltpu.VMEM(((2 * REACH + 1) * rows, width), jnp.bfloat16),
        pltpu.VMEM((here, MOST, BLOCK, BLOCK), jnp.float32),
        pltpu.VMEM((here * MOST, BLOCK), jnp.float32),
        pltpu.VMEM((here * MOST, BLOCK), jnp.float32),
    ]
    args = [info, *slabs]
    in_specs = [scalar] + [pl.BlockSpec(memory_space=pl.ANY)] * len(slabs)
    out_shape, scratch = list(state_shape), []
    if last:
        args.append(shifts)
        in_specs.append(whole)
        out_shape = [
            jax.ShapeDtypeStruct((here, BLOCK), jnp.float32),
            jax.ShapeDtypeStruct((rows, width), jnp.float32),
        ] + out_shape
        scratch = [
            pltpu.VMEM((MOST, BLOCK), jnp.float32),
            pltpu.VMEM((BLOCK, MOST * BLOCK), jnp.bfloat16),
        ]
    aliases = {}
    if not first:
        aliases = {len(args) + n: len(out_shape) - len(state) + n for n in range(len(state))}
        args.extend(state)
        in_specs.extend([whole] * len(state))

    def body(*refs):
        stage(here, new_slots, prior_slots, first, last, refs)

    return pl.pallas_call(
        body,
        out_shape=tuple(out_shape),
        in_specs=in_specs,
        out_specs=tuple([whole] * len(out_shape)),
        scratch_shapes=[
            pltpu.VMEM((MOST * BLOCK, BLOCK), jnp.float32),
            pltpu.SemaphoreType.DMA((len(slabs),)),
        ]
        + scratch,
        input_output_aliases=aliases,
        compiler_params=pltpu.CompilerParams(vmem_limit_bytes=24 * 1024 * 1024),
        name="cluster_loss" if last else "cluster_scores",
    )(*args)


STAGES = ((0, 1, 2, 3, 4, 5), (6,), (7, 8, 9))


def cluster_extents(device, block_cluster, here):
    margin = jnp.full((REACH * here,), -1, jnp.int32)
    padded = jnp.concatenate([margin, block_cluster, margin])
    near = lax.dynamic_slice_in_dim(padded, device * here, (2 * REACH + 1) * here)
    info = [device]
    for own in (REACH * here, REACH * here + 1):
        mine = near == near[own]
        info.append(own - jnp.sum(mine[own - MOST + 1 : own]))
        info.append(own + 1 + jnp.sum(mine[own + 1 : own + MOST]))
    return jnp.stack(info + [device] * 3).astype(jnp.int32)


def local_work(info, shifts, slabs):
    rows = slabs[0].shape[0]
    state, prior = None, ()
    for new in STAGES[:-1]:
        state = run_stage(info, [slabs[n] for n in new], new, prior, state, None)
        prior = prior + new
    new = STAGES[-1]
    loss, grad, *_ = run_stage(info, [slabs[n] for n in new], new, prior, state, shifts)
    return loss.reshape(rows), grad


def shards(embeddings, block_cluster, partner_shift):
    here = embeddings.shape[0] // BLOCK
    device = lax.axis_index(AXES).astype(jnp.int32)
    info = cluster_extents(device, block_cluster, here)
    slabs, (info, shifts) = exchange(embeddings, info, partner_shift.reshape(here, BLOCK))
    return local_work(info, shifts, slabs)


def solution(mesh):
    in_specs = (P(AXES, None), P(), P(AXES))
    out_specs = (P(AXES), P(AXES, None))
    return jax.shard_map(shards, mesh=mesh, in_specs=in_specs, out_specs=out_specs, check_vma=False)
```

```python
import functools
import math

import jax
import jax.numpy as jnp
from jax import lax
from jax.experimental import pallas as pl
from jax.experimental.pallas import tpu as pltpu
from jax.sharding import PartitionSpec as P

BLOCK = 256
REACH = 4
LINE = 4
LANES = 128
MOST = 8
NEG = -1e30
AXES = ("row", "col")


def moved(value, target, cyclic=True):
    count = lax.axis_size(AXES)
    pairs = [(source, target(source // LINE, source % LINE)) for source in range(count)]
    pairs = [(source, to[0] * LINE + to[1]) for source, to in pairs if to is not None]
    if not cyclic:
        pairs = [(source, to) for source, to in pairs if 0 <= to < count]
    return lax.ppermute(value, AXES, [(source, to % count) for source, to in pairs])


def parity(line):
    return line // 2 % 2


def exchange(own, info, shifts):
    late = moved(own, lambda line, at: (line + 1 if at == LINE - 1 else line - 1, at))
    near = moved(own, lambda line, at: (line, (at + (1 if (at + parity(line)) % 2 else -1)) % LINE))
    other = moved(own, lambda line, at: (line, (at - (1 if (at + parity(line)) % 2 else -1)) % LINE))
    across = moved(near, lambda line, at: (line, (at - (1 if (at + parity(line)) % 2 else -1)) % LINE))
    state = run_stage(info, [own, near], STAGES[0], (), None, None)
    late_sent, shifts, _ = lax.optimization_barrier((late, shifts, state[3]))
    early = moved(late_sent, lambda line, at: (line - 2 if at == LINE - 1 else line + 2, at))
    late_up = moved(late, lambda line, at: (line, (at + 1) % LINE))
    late_down = moved(late, lambda line, at: (line, at - 1) if at == 3 else (line, 3) if at == 0 else None)
    early_down = moved(early, lambda line, at: (line, at - 1) if at in (1, 2) else None)
    crossed = moved(
        across, lambda line, at: (line - 1 if at >= 2 else line + 1, at), cyclic=False
    )
    slabs = [own, late, early, across, near, other, crossed, late_up, late_down, early_down]
    return slabs, state, shifts


def slots(device):
    at = lax.rem(device, LINE)
    late = jnp.where(at < 3, 8, 0)
    across = jnp.where(at >= 2, 2, 6)
    from_before = jnp.where(at >= 1, 3, 7)
    from_after = jnp.where(at <= 2, 5, 1)
    before = lax.rem(at + lax.rem(lax.div(device, 2 * LINE), 2), 2) == 0
    near = jnp.where(before, from_before, from_after)
    other = jnp.where(before, from_after, from_before)
    down = 6 - from_after
    where = [4, late, 8 - late, across, near, other, 8 - across, 10 - from_before, down, down]
    return where, [None] * 8 + [at >= 2, at < 2]


def stage(here, new_slots, prior_slots, first, last, refs):
    info_ref, refs = refs[0], refs[1:]
    slabs, refs = refs[: len(new_slots)], refs[len(new_slots) :]
    if last:
        shift_ref, refs = refs[0], refs[1:]
    if not first:
        refs = refs[4:]
    if last:
        loss_ref, grad_ref, refs = refs[0], refs[1], refs[2:]
    window, kept, tops, totals, scores, top_ref, total_ref, sems = refs[:8]
    if last:
        lse, weights = refs[8], refs[9:]
    rows, width = slabs[0].shape
    scale = width**-0.5
    log2e = math.log2(math.e)
    size = MOST // 2 if first else MOST
    all_slots, taken = slots(info_ref[0])
    copies = [
        pltpu.make_async_copy(
            slab,
            window.at[pl.ds(pl.multiple_of(all_slots[n] * rows, rows), rows), :],
            sems.at[k],
        )
        for k, (slab, n) in enumerate(zip(slabs, new_slots))
    ]
    copies = [(taken[n], copy) for n, copy in zip(new_slots, copies)]

    def each(act):
        for wanted, copy in copies:
            if wanted is None:
                act(copy)
            else:
                pl.when(wanted)(lambda copy=copy: act(copy))

    each(lambda copy: copy.start())

    def mask_of(ids):
        mask = jnp.int32(0)
        for n in ids:
            bit = lax.shift_left(jnp.int32(1), jnp.int32(all_slots[n]))
            if taken[n] is not None:
                bit = jnp.where(taken[n], bit, 0)
            mask = jnp.bitwise_or(mask, bit)
        return mask

    new_mask, prior_mask = mask_of(new_slots), mask_of(prior_slots)

    def held(mask, w):
        return jnp.bitwise_and(lax.shift_right_logical(mask, lax.div(w, here)), 1) == 1

    begin0, end0, begin1, end1 = [info_ref[n] for n in range(1, 5)]
    each(lambda copy: copy.wait())

    row = lax.broadcasted_iota(jnp.int32, (BLOCK, BLOCK), 0)
    column = lax.broadcasted_iota(jnp.int32, (BLOCK, BLOCK), 1)
    span = MOST * BLOCK
    same = begin0 == begin1

    def at(block):
        return pl.ds(pl.multiple_of(block * BLOCK, BLOCK), BLOCK)

    def folded(op, tile):
        return op(tile.reshape(BLOCK // 8, 8, BLOCK), axis=0)

    def upright(values):
        return jnp.sum(jnp.where(row == column, values, 0.0), axis=1, keepdims=True)

    def product(left, right):
        return lax.dot_general(
            window[at(left), :],
            window[at(right), :],
            (((1,), (1,)), ((), ())),
            preferred_element_type=jnp.float32,
        ) * (scale * log2e)

    def own_block(r, _):
        begin = jnp.where(r == 0, begin0, begin1)
        length = jnp.where(r == 0, end0, end1) - begin
        own = REACH * here + r - begin

        def live(i, mask):
            return jnp.logical_and(i < length, held(mask, begin + i))

        def column_strip(j, _):
            def part_of_strip(chunk):
                top, total = top_ref[...], total_ref[...]
                lines = pl.ds(pl.multiple_of(r * MOST, MOST), MOST)
                olds, sums, new_tops, new_sums = tops[lines, :], totals[lines, :], [], []
                for i in range(chunk * size, (chunk + 1) * size):
                    tile = product(begin + i, begin + j)
                    tile = jnp.where(row + (i - j) * (2 * BLOCK) == column, NEG, tile)
                    scores[i * BLOCK : (i + 1) * BLOCK, :] = tile
                    there = live(i, new_mask + prior_mask)
                    high = jnp.max(folded(jnp.max, tile), axis=0, keepdims=True)
                    high = jnp.where(there, jnp.maximum(top, high), top)
                    part = folded(jnp.sum, jnp.exp2(tile - high))
                    total = total * jnp.exp2(top - high)
                    total = jnp.where(there, total + part, total)
                    top = high
                    if first:
                        continue
                    there = live(i, prior_mask)
                    flipped = tile.T
                    old = olds[i : i + 1, :]
                    high = jnp.max(folded(jnp.max, flipped), axis=0, keepdims=True)
                    high = jnp.maximum(old, high)
                    part = jnp.sum(folded(jnp.sum, jnp.exp2(flipped - high)), axis=0, keepdims=True)
                    part = sums[i : i + 1, :] * jnp.exp2(old - high) + part
                    new_sums.append(jnp.where(there, part, sums[i : i + 1, :]))
                    new_tops.append(jnp.where(there, high, old))
                if not first:
                    totals[lines, :] = jnp.concatenate(new_sums, axis=0)
                    tops[lines, :] = jnp.concatenate(new_tops, axis=0)
                top_ref[...] = top
                total_ref[...] = total

            @pl.when(held(new_mask, begin + j))
            def _():
                top_ref[...] = jnp.full((1, BLOCK), NEG, jnp.float32)
                total_ref[...] = jnp.zeros((8, BLOCK), jnp.float32)
                for chunk in range(MOST // size):
                    some = False
                    for i in range(chunk * size, (chunk + 1) * size):
                        some = jnp.logical_or(some, live(i, new_mask + prior_mask))
                    pl.when(some)(lambda chunk=chunk: part_of_strip(chunk))
                tops[pl.ds(r * MOST + j, 1), :] = top_ref[...]
                totals[pl.ds(r * MOST + j, 1), :] = jnp.sum(total_ref[...], axis=0, keepdims=True)
                kept[r, j] = scores[at(own), :]

                @pl.when(same)
                def _():
                    kept[1, j] = scores[at(own + 1), :]

            return 0

        @pl.when(jnp.logical_or(r == 0, jnp.logical_not(same)))
        def _():
            lax.fori_loop(0, length, column_strip, 0)

        return 0

    lax.fori_loop(0, here, own_block, 0)
    if not last:
        return

    def weigh(r):
        begin, end = ((begin0, end0), (begin1, end1))[r]
        own = REACH * here + r - begin
        ready = pl.ds(pl.multiple_of(jnp.where(same, 0, r * MOST), MOST), MOST)
        lse[...] = tops[ready, :] + jnp.log2(totals[ready, :])
        mine = lse[pl.ds(own, 1), :]
        mine_up = upright(mine)
        for j in range(MOST):
            tile = kept[r, j]
            weight = jnp.exp2(tile - mine_up) + jnp.exp2(tile - lse[j : j + 1, :])
            weight = jnp.where(j < end - begin, weight, 0.0)
            weights[r][:, j * BLOCK : (j + 1) * BLOCK] = weight.astype(jnp.bfloat16)
        shift = shift_ref[r : r + 1, :]
        shift_up = upright(shift.astype(jnp.float32)).astype(jnp.int32)
        tile = kept[r, own]
        behind = row == jnp.bitwise_and(column + shift, BLOCK - 1)
        ahead = column == jnp.bitwise_and(row + shift_up, BLOCK - 1)
        weight = jnp.exp2(tile - mine_up) + jnp.exp2(tile - mine)
        weight = weight - jnp.where(ahead, 1.0, 0.0) - jnp.where(behind, 1.0, 0.0)
        weights[r][:, at(own)] = weight.astype(jnp.bfloat16)
        positive = jnp.sum(jnp.where(behind, tile, 0.0), axis=0, keepdims=True)
        loss = (mine - positive) * (1.0 / log2e)
        for n in range(BLOCK // LANES):
            k = r * (BLOCK // LANES) + n
            loss_ref[k : k + 1, :] = loss[:, n * LANES : (n + 1) * LANES]

    def spread(r):
        begin = (begin0, begin1)[r]
        total = jnp.dot(
            weights[r][...],
            window[pl.ds(pl.multiple_of(begin * BLOCK, BLOCK), span), :],
            preferred_element_type=jnp.float32,
        )
        grad_ref[r * BLOCK : (r + 1) * BLOCK, :] = total * scale

    for r in range(here):
        weigh(r)
        spread(r)


def run_stage(info, slabs, new_slots, prior_slots, state, shifts):
    rows, width = slabs[0].shape
    here = rows // BLOCK
    first, last = state is None, shifts is not None
    whole = pl.BlockSpec(memory_space=pltpu.VMEM)
    scalar = pl.BlockSpec(memory_space=pltpu.SMEM)
    state_shape = [
        pltpu.VMEM(((2 * REACH + 1) * rows, width), jnp.bfloat16),
        pltpu.VMEM((here, MOST, BLOCK, BLOCK), jnp.float32),
        pltpu.VMEM((here * MOST, BLOCK), jnp.float32),
        pltpu.VMEM((here * MOST, BLOCK), jnp.float32),
    ]
    args = [info, *slabs]
    in_specs = [scalar] + [pl.BlockSpec(memory_space=pl.ANY)] * len(slabs)
    out_shape, scratch = list(state_shape), []
    if last:
        args.append(shifts)
        in_specs.append(whole)
        out_shape = [
            jax.ShapeDtypeStruct((rows // LANES, LANES), jnp.float32),
            jax.ShapeDtypeStruct((rows, width), jnp.float32),
        ] + out_shape
        scratch = [
            pltpu.VMEM((MOST, BLOCK), jnp.float32),
        ] + [pltpu.VMEM((BLOCK, MOST * BLOCK), jnp.bfloat16)] * here
    aliases = {}
    if not first:
        aliases = {len(args) + n: len(out_shape) - len(state) + n for n in range(len(state))}
        args.extend(state)
        in_specs.extend([whole] * len(state))

    def body(*refs):
        stage(here, new_slots, prior_slots, first, last, refs)

    return pl.pallas_call(
        body,
        out_shape=tuple(out_shape),
        in_specs=in_specs,
        out_specs=tuple([whole] * len(out_shape)),
        scratch_shapes=[
            pltpu.VMEM((MOST * BLOCK, BLOCK), jnp.float32),
            pltpu.VMEM((1, BLOCK), jnp.float32),
            pltpu.VMEM((8, BLOCK), jnp.float32),
            pltpu.SemaphoreType.DMA((len(slabs),)),
        ]
        + scratch,
        input_output_aliases=aliases,
        compiler_params=pltpu.CompilerParams(vmem_limit_bytes=24 * 1024 * 1024),
        name="cluster_loss" if last else "cluster_scores",
    )(*args)


STAGES = ((0, 4), (1, 2, 3, 5), (7, 8), (6,), (9,))


def cluster_extents(device, block_cluster, here):
    margin = jnp.full((REACH * here,), -1, jnp.int32)
    padded = jnp.concatenate([margin, block_cluster, margin])
    near = lax.dynamic_slice_in_dim(padded, device * here, (2 * REACH + 1) * here)
    info = [device]
    for own in (REACH * here, REACH * here + 1):
        mine = near == near[own]
        info.append(own - jnp.sum(mine[own - MOST + 1 : own]))
        info.append(own + 1 + jnp.sum(mine[own + 1 : own + MOST]))
    return jnp.stack(info + [device] * 3).astype(jnp.int32)


def local_work(info, shifts, slabs, state):
    rows = slabs[0].shape[0]
    prior = STAGES[0]
    for new in STAGES[1:-1]:
        state = run_stage(info, [slabs[n] for n in new], new, prior, state, None)
        prior = prior + new
    new = STAGES[-1]
    loss, grad, *_ = run_stage(info, [slabs[n] for n in new], new, prior, state, shifts)
    return loss.reshape(rows), grad


def shards(embeddings, block_cluster, partner_shift):
    here = embeddings.shape[0] // BLOCK
    device = lax.axis_index(AXES).astype(jnp.int32)
    info = cluster_extents(device, block_cluster, here)
    slabs, state, shifts = exchange(embeddings, info, partner_shift.reshape(here, BLOCK))
    return local_work(info, shifts, slabs, state)


def solution(mesh):
    in_specs = (P(AXES, None), P(), P(AXES))
    out_specs = (P(AXES), P(AXES, None))
    return jax.shard_map(shards, mesh=mesh, in_specs=in_specs, out_specs=out_specs, check_vma=False)
```

```python
import functools
import math

import jax
import jax.numpy as jnp
from jax import lax
from jax.experimental import pallas as pl
from jax.experimental.pallas import tpu as pltpu
from jax.sharding import PartitionSpec as P

BLOCK = 256
REACH = 4
LINE = 4
LANES = 128
MOST = 8
NEG = -1e30
AXES = ("row", "col")


def moved(value, target, cyclic=True):
    count = lax.axis_size(AXES)
    pairs = [(source, target(source // LINE, source % LINE)) for source in range(count)]
    pairs = [(source, to[0] * LINE + to[1]) for source, to in pairs if to is not None]
    if not cyclic:
        pairs = [(source, to) for source, to in pairs if 0 <= to < count]
    return lax.ppermute(value, AXES, [(source, to % count) for source, to in pairs])


def parity(line):
    return line // 2 % 2


def exchange(own, info, shifts):
    late = moved(own, lambda line, at: (line + 1 if at == LINE - 1 else line - 1, at))
    near = moved(own, lambda line, at: (line, (at + (1 if (at + parity(line)) % 2 else -1)) % LINE))
    other = moved(own, lambda line, at: (line, (at - (1 if (at + parity(line)) % 2 else -1)) % LINE))
    across = moved(near, lambda line, at: (line, (at - (1 if (at + parity(line)) % 2 else -1)) % LINE))
    state = run_stage(info, [own, near], STAGES[0], (), None, None)
    late_sent, shifts, _ = lax.optimization_barrier((late, shifts, state[3]))
    early = moved(late_sent, lambda line, at: (line - 2 if at == LINE - 1 else line + 2, at))
    late_up = moved(late, lambda line, at: (line, (at + 1) % LINE))
    late_down = moved(late, lambda line, at: (line, at - 1) if at == 3 else (line, 3) if at == 0 else None)
    early_down = moved(early, lambda line, at: (line, at - 1) if at in (1, 2) else None)
    crossed = moved(
        across, lambda line, at: (line - 1 if at >= 2 else line + 1, at), cyclic=False
    )
    slabs = [own, late, early, across, near, other, crossed, late_up, late_down, early_down]
    return slabs, state, shifts


def slots(device):
    at = lax.rem(device, LINE)
    late = jnp.where(at < 3, 8, 0)
    across = jnp.where(at >= 2, 2, 6)
    from_before = jnp.where(at >= 1, 3, 7)
    from_after = jnp.where(at <= 2, 5, 1)
    before = lax.rem(at + lax.rem(lax.div(device, 2 * LINE), 2), 2) == 0
    near = jnp.where(before, from_before, from_after)
    other = jnp.where(before, from_after, from_before)
    down = 6 - from_after
    where = [4, late, 8 - late, across, near, other, 8 - across, 10 - from_before, down, down]
    return where, [None] * 8 + [at >= 2, at < 2]


def stage(here, new_slots, prior_slots, first, last, refs):
    info_ref, refs = refs[0], refs[1:]
    slabs, refs = refs[: len(new_slots)], refs[len(new_slots) :]
    if last:
        shift_ref, refs = refs[0], refs[1:]
    if not first:
        refs = refs[4:]
    if last:
        loss_ref, grad_ref, refs = refs[0], refs[1], refs[2:]
    window, kept, tops, totals, scores, top_ref, total_ref, sems = refs[:8]
    if last:
        lse, weights = refs[8], refs[9:]
    rows, width = slabs[0].shape
    scale = width**-0.5
    log2e = math.log2(math.e)
    size = MOST // 2 if first else MOST
    all_slots, taken = slots(info_ref[0])
    copies = [
        pltpu.make_async_copy(
            slab,
            window.at[pl.ds(pl.multiple_of(all_slots[n] * rows, rows), rows), :],
            sems.at[k],
        )
        for k, (slab, n) in enumerate(zip(slabs, new_slots))
    ]
    copies = [(taken[n], copy) for n, copy in zip(new_slots, copies)]

    def each(act):
        for wanted, copy in copies:
            if wanted is None:
                act(copy)
            else:
                pl.when(wanted)(lambda copy=copy: act(copy))

    each(lambda copy: copy.start())

    def mask_of(ids):
        mask = jnp.int32(0)
        for n in ids:
            bit = lax.shift_left(jnp.int32(1), jnp.int32(all_slots[n]))
            if taken[n] is not None:
                bit = jnp.where(taken[n], bit, 0)
            mask = jnp.bitwise_or(mask, bit)
        return mask

    new_mask, prior_mask = mask_of(new_slots), mask_of(prior_slots)

    def held(mask, w):
        return jnp.bitwise_and(lax.shift_right_logical(mask, lax.div(w, here)), 1) == 1

    begin0, end0, begin1, end1 = [info_ref[n] for n in range(1, 5)]
    each(lambda copy: copy.wait())

    row = lax.broadcasted_iota(jnp.int32, (BLOCK, BLOCK), 0)
    column = lax.broadcasted_iota(jnp.int32, (BLOCK, BLOCK), 1)
    span = MOST * BLOCK
    same = begin0 == begin1

    def at(block):
        return pl.ds(pl.multiple_of(block * BLOCK, BLOCK), BLOCK)

    def folded(op, tile):
        return op(tile.reshape(BLOCK // 8, 8, BLOCK), axis=0)

    def upright(values):
        return jnp.sum(jnp.where(row == column, values, 0.0), axis=1, keepdims=True)

    def product(left, right):
        return lax.dot_general(
            window[at(left), :],
            window[at(right), :],
            (((1,), (1,)), ((), ())),
            preferred_element_type=jnp.float32,
        ) * (scale * log2e)

    def own_block(r, _):
        begin = jnp.where(r == 0, begin0, begin1)
        length = jnp.where(r == 0, end0, end1) - begin
        own = REACH * here + r - begin

        def live(i, mask):
            return jnp.logical_and(i < length, held(mask, begin + i))

        def column_strip(j, _):
            def part_of_strip(chunk):
                top, total = top_ref[...], total_ref[...]
                lines = pl.ds(pl.multiple_of(r * MOST, MOST), MOST)
                olds, sums, new_tops, new_sums = tops[lines, :], totals[lines, :], [], []
                for i in range(chunk * size, (chunk + 1) * size):
                    tile = product(begin + i, begin + j)
                    tile = jnp.where(row + (i - j) * (2 * BLOCK) == column, NEG, tile)
                    scores[i * BLOCK : (i + 1) * BLOCK, :] = tile
                    there = live(i, new_mask + prior_mask)
                    high = jnp.max(folded(jnp.max, tile), axis=0, keepdims=True)
                    high = jnp.where(there, jnp.maximum(top, high), top)
                    part = folded(jnp.sum, jnp.exp2(tile - high))
                    total = total * jnp.exp2(top - high)
                    total = jnp.where(there, total + part, total)
                    top = high
                    if first:
                        continue
                    there = live(i, prior_mask)
                    flipped = tile.T
                    old = olds[i : i + 1, :]
                    high = jnp.max(folded(jnp.max, flipped), axis=0, keepdims=True)
                    high = jnp.maximum(old, high)
                    part = jnp.sum(folded(jnp.sum, jnp.exp2(flipped - high)), axis=0, keepdims=True)
                    part = sums[i : i + 1, :] * jnp.exp2(old - high) + part
                    new_sums.append(jnp.where(there, part, sums[i : i + 1, :]))
                    new_tops.append(jnp.where(there, high, old))
                if not first:
                    totals[lines, :] = jnp.concatenate(new_sums, axis=0)
                    tops[lines, :] = jnp.concatenate(new_tops, axis=0)
                top_ref[...] = top
                total_ref[...] = total

            @pl.when(held(new_mask, begin + j))
            def _():
                top_ref[...] = jnp.full((1, BLOCK), NEG, jnp.float32)
                total_ref[...] = jnp.zeros((8, BLOCK), jnp.float32)
                for chunk in range(MOST // size):
                    some = False
                    for i in range(chunk * size, (chunk + 1) * size):
                        some = jnp.logical_or(some, live(i, new_mask + prior_mask))
                    pl.when(some)(lambda chunk=chunk: part_of_strip(chunk))
                tops[pl.ds(r * MOST + j, 1), :] = top_ref[...]
                totals[pl.ds(r * MOST + j, 1), :] = jnp.sum(total_ref[...], axis=0, keepdims=True)
                kept[r, j] = scores[at(own), :]

                @pl.when(same)
                def _():
                    kept[1, j] = scores[at(own + 1), :]

            return 0

        @pl.when(jnp.logical_or(r == 0, jnp.logical_not(same)))
        def _():
            lax.fori_loop(0, length, column_strip, 0)

        return 0

    lax.fori_loop(0, here, own_block, 0)
    if not last:
        return

    def weigh(r):
        begin, end = ((begin0, end0), (begin1, end1))[r]
        own = REACH * here + r - begin
        ready = pl.ds(pl.multiple_of(jnp.where(same, 0, r * MOST), MOST), MOST)
        lse[...] = tops[ready, :] + jnp.log2(totals[ready, :])
        mine = lse[pl.ds(own, 1), :]
        mine_up = upright(mine)
        for j in range(MOST):
            tile = kept[r, j]
            weight = jnp.exp2(tile - mine_up) + jnp.exp2(tile - lse[j : j + 1, :])
            weight = jnp.where(j < end - begin, weight, 0.0)
            weights[r][:, j * BLOCK : (j + 1) * BLOCK] = weight.astype(jnp.bfloat16)
        shift = shift_ref[r : r + 1, :]
        shift_up = upright(shift.astype(jnp.float32)).astype(jnp.int32)
        tile = kept[r, own]
        behind = row == jnp.bitwise_and(column + shift, BLOCK - 1)
        ahead = column == jnp.bitwise_and(row + shift_up, BLOCK - 1)
        weight = jnp.exp2(tile - mine_up) + jnp.exp2(tile - mine)
        weight = weight - jnp.where(ahead, 1.0, 0.0) - jnp.where(behind, 1.0, 0.0)
        weights[r][:, at(own)] = weight.astype(jnp.bfloat16)
        positive = jnp.sum(jnp.where(behind, tile, 0.0), axis=0, keepdims=True)
        loss = (mine - positive) * (1.0 / log2e)
        for n in range(BLOCK // LANES):
            k = r * (BLOCK // LANES) + n
            loss_ref[k : k + 1, :] = loss[:, n * LANES : (n + 1) * LANES]

    def spread(r):
        begin = (begin0, begin1)[r]
        total = jnp.dot(
            weights[r][...],
            window[pl.ds(pl.multiple_of(begin * BLOCK, BLOCK), span), :],
            preferred_element_type=jnp.float32,
        )
        grad_ref[r * BLOCK : (r + 1) * BLOCK, :] = total * scale

    for r in range(here):
        weigh(r)
        spread(r)


def run_stage(info, slabs, new_slots, prior_slots, state, shifts):
    rows, width = slabs[0].shape
    here = rows // BLOCK
    first, last = state is None, shifts is not None
    whole = pl.BlockSpec(memory_space=pltpu.VMEM)
    scalar = pl.BlockSpec(memory_space=pltpu.SMEM)
    state_shape = [
        pltpu.VMEM(((2 * REACH + 1) * rows, width), jnp.bfloat16),
        pltpu.VMEM((here, MOST, BLOCK, BLOCK), jnp.float32),
        pltpu.VMEM((here * MOST, BLOCK), jnp.float32),
        pltpu.VMEM((here * MOST, BLOCK), jnp.float32),
    ]
    args = [info, *slabs]
    in_specs = [scalar] + [pl.BlockSpec(memory_space=pl.ANY)] * len(slabs)
    out_shape, scratch = list(state_shape), []
    if last:
        args.append(shifts)
        in_specs.append(whole)
        out_shape = [
            jax.ShapeDtypeStruct((rows // LANES, LANES), jnp.float32),
            jax.ShapeDtypeStruct((rows, width), jnp.float32),
        ] + out_shape
        scratch = [
            pltpu.VMEM((MOST, BLOCK), jnp.float32),
        ] + [pltpu.VMEM((BLOCK, MOST * BLOCK), jnp.bfloat16)] * here
    aliases = {}
    if not first:
        aliases = {len(args) + n: len(out_shape) - len(state) + n for n in range(len(state))}
        args.extend(state)
        in_specs.extend([whole] * len(state))

    def body(*refs):
        stage(here, new_slots, prior_slots, first, last, refs)

    return pl.pallas_call(
        body,
        out_shape=tuple(out_shape),
        in_specs=in_specs,
        out_specs=tuple([whole] * len(out_shape)),
        scratch_shapes=[
            pltpu.VMEM((MOST * BLOCK, BLOCK), jnp.float32),
            pltpu.VMEM((1, BLOCK), jnp.float32),
            pltpu.VMEM((8, BLOCK), jnp.float32),
            pltpu.SemaphoreType.DMA((len(slabs),)),
        ]
        + scratch,
        input_output_aliases=aliases,
        compiler_params=pltpu.CompilerParams(vmem_limit_bytes=24 * 1024 * 1024),
        name="cluster_loss" if last else "cluster_scores",
    )(*args)


STAGES = ((0, 4), (1, 2, 3, 5), (8,), (7,), (6,), (9,))


def cluster_extents(device, block_cluster, here):
    margin = jnp.full((REACH * here,), -1, jnp.int32)
    padded = jnp.concatenate([margin, block_cluster, margin])
    near = lax.dynamic_slice_in_dim(padded, device * here, (2 * REACH + 1) * here)
    info = [device]
    for own in (REACH * here, REACH * here + 1):
        mine = near == near[own]
        info.append(own - jnp.sum(mine[own - MOST + 1 : own]))
        info.append(own + 1 + jnp.sum(mine[own + 1 : own + MOST]))
    return jnp.stack(info + [device] * 3).astype(jnp.int32)


def local_work(info, shifts, slabs, state):
    rows = slabs[0].shape[0]
    prior = STAGES[0]
    for new in STAGES[1:-1]:
        state = run_stage(info, [slabs[n] for n in new], new, prior, state, None)
        prior = prior + new
    new = STAGES[-1]
    loss, grad, *_ = run_stage(info, [slabs[n] for n in new], new, prior, state, shifts)
    return loss.reshape(rows), grad


def shards(embeddings, block_cluster, partner_shift):
    here = embeddings.shape[0] // BLOCK
    device = lax.axis_index(AXES).astype(jnp.int32)
    info = cluster_extents(device, block_cluster, here)
    slabs, state, shifts = exchange(embeddings, info, partner_shift.reshape(here, BLOCK))
    return local_work(info, shifts, slabs, state)


def solution(mesh):
    in_specs = (P(AXES, None), P(), P(AXES))
    out_specs = (P(AXES), P(AXES, None))
    return jax.shard_map(shards, mesh=mesh, in_specs=in_specs, out_specs=out_specs, check_vma=False)
```
